256 devices in a mesh: outer: 8 (over z), inner: 32 (over y, x, core).
Axes of the slice: x: 4, y: 4, z: 8, core: 2. Of those that a mesh axis runs over, the one named last changes fastest.
Arguments:
- queries: bfloat16 [262144, 1024], P(('outer', 'inner')), may hold values from -6 to 6
- keys: bfloat16 [262144, 1024], P(('outer', 'inner')), may hold values from -0.5 to 0.5
- values: bfloat16 [262144, 1024], P(('outer', 'inner')), may hold values from -6 to 6
- level_weights: float32 [19, 8, 262144], P(None, None, ('outer', 'inner')), as said below
- out_weight: bfloat16 [1024, 1024], replicated, may hold values from -0.046875 to 0.046875
Outputs:
- mixed: bfloat16 [262144, 1024], P(('outer', 'inner'))
The draws below stay inside these ranges and needn't reach their ends.
Inputs may be any that keep to these rules, and one draw needn't show every extreme that they name: `level_weights`: every entry is positive.
All inputs are finite; a program needn't handle non-finite values.
Results may differ from the reference program's by a relative error of at most 0.0057.
Values sent between devices are 32-bit elements; how exact they have to be, the bound alone decides.
A program may use at most 128 MiB of HBM per device.

```python
import jax
import jax.numpy as jnp
from jax import lax

HEADS = 8
HEAD = 128
D = 1024
TOK_DEV = 1024
TOKENS = 262144
LOCAL_BITS = 10
INNER_BITS = 5
OUTER_BITS = 3
LEVELS = 19
N_OUTER = 8
N_INNER = 32


def draw_level_weights(key, part):
    level_index = jnp.arange(LEVELS).astype(jnp.float32)
    level_scale = 2.0 ** (-jnp.maximum(level_index - 1.0, 0.0) / 2.0)
    shape = (LEVELS, HEADS, TOKENS)
    factor = jnp.exp(jax.random.uniform(key, shape, jnp.float32, jnp.log(0.5), jnp.log(2.0)))
    return (factor * level_scale[:, None, None]).astype(jnp.float32)


def shard_levels(stream_key, extent, split, least, largest):
    def one(dim, shards_of):
        draws = jax.random.uniform(jax.random.fold_in(jax.random.fold_in(stream_key, 6), dim), (shards_of,), jnp.float32, least / len(split), largest / len(split))
        return jnp.repeat(jnp.exp(draws), extent[dim] // shards_of).reshape((-1,) + (1,) * (len(extent) - dim - 1))

    loudness = one(*split[0])
    for cut in split[1:]:
        loudness = loudness * one(*cut)
    return loudness


def gaussian(stream_key, shape, spread, bound, cuts=(), kind=jnp.bfloat16):
    entries = jax.random.normal(stream_key, shape, jnp.float32) * spread
    if len(cuts) > 0:
        entries = shard_levels(stream_key, shape, cuts, -0.22, 0.18) * entries
    return jnp.clip(entries, min=-bound, max=bound).astype(kind)


def setup_inputs(seed: int = 0) -> dict:
    seeds = jax.random.split(jax.random.key(seed), 6)
    return {
        "queries": gaussian(seeds[0], (TOKENS, D), 1.0, 6.0, ((0, 256),)),
        "keys": gaussian(seeds[1], (TOKENS, D), 0.088, 0.5, ((0, 256),)),
        "values": gaussian(seeds[2], (TOKENS, D), 1.0, 6.0, ((0, 256),)),
        "level_weights": draw_level_weights(jax.random.fold_in(seeds[5], 71), 0),
        "out_weight": gaussian(seeds[4], (D, D), (16 * D) ** -0.5, 0.046875),
    }


def level_onehot(row_count, local_bits):
    target = lax.iota(jnp.int32, row_count)[:, None]
    source = lax.iota(jnp.int32, row_count)[None, :]
    differ = jnp.bitwise_xor(target, source)
    level = jnp.zeros((row_count, row_count), jnp.int32)
    for shift in range(local_bits):
        level = level + (jnp.right_shift(differ, shift) > 0).astype(jnp.int32)
    picks = lax.iota(jnp.int32, local_bits + 1)[:, None, None]
    return jnp.logical_and(level[None] == picks, (source <= target)[None]).astype(jnp.float32)


def reference(queries, keys, values, level_weights, out_weight):
    block_count = N_OUTER * N_INNER
    dev_bits = INNER_BITS + OUTER_BITS
    query_blocks = queries.reshape(block_count, TOK_DEV, HEADS, HEAD)
    key_blocks = keys.reshape(block_count, TOK_DEV, HEADS, HEAD)
    value_blocks = values.reshape(block_count, TOK_DEV, HEADS, HEAD)
    lam_blocks = jnp.transpose(level_weights.reshape(LEVELS, HEADS, block_count, TOK_DEV), (2, 0, 1, 3))

    def state_of(pair):
        return jnp.einsum("the,thf->hef", pair[0].astype(jnp.float32), pair[1].astype(jnp.float32),
                          precision=lax.Precision.HIGHEST)

    states = lax.map(state_of, (key_blocks, value_blocks))
    groups = [states]
    running = states
    for level_bit in range(dev_bits - 1):
        running = running[0::2] + running[1::2]
        groups.append(running)
    onehot = level_onehot(TOK_DEV, LOCAL_BITS)

    def one_block(block_index):
        query_here = query_blocks[block_index].astype(jnp.float32)
        key_here = key_blocks[block_index].astype(jnp.float32)
        value_here = value_blocks[block_index].astype(jnp.float32)
        lam_here = lam_blocks[block_index]
        mixing = jnp.einsum("lts,lht->hts", onehot, lam_here[:LOCAL_BITS + 1], precision=lax.Precision.HIGHEST)
        scores = jnp.einsum("the,she->hts", query_here, key_here, precision=lax.Precision.HIGHEST)
        weighted = (scores * mixing).astype(jnp.bfloat16).astype(jnp.float32)
        local_part = jnp.einsum("hts,she->the", weighted, value_here, precision=lax.Precision.HIGHEST)
        buckets = []
        for level_bit in range(dev_bits):
            position = jnp.right_shift(block_index, level_bit)
            upper_half = jnp.bitwise_and(position, 1) == 1
            lower_state = lax.dynamic_index_in_dim(groups[level_bit], jnp.bitwise_xor(position, 1), 0, keepdims=False)
            buckets.append(jnp.where(upper_half, lower_state, jnp.zeros_like(lower_state)))
        stacked = jnp.stack(buckets).astype(jnp.bfloat16).astype(jnp.float32)
        products = jnp.einsum("the,lhef->lthf", query_here, stacked, precision=lax.Precision.HIGHEST)
        remote_lam = jnp.transpose(lam_here[LOCAL_BITS + 1:], (0, 2, 1))[:, :, :, None]
        remote_part = jnp.sum(products * remote_lam, axis=0)
        attended = (local_part + remote_part).astype(jnp.bfloat16).reshape(TOK_DEV, HEADS * HEAD)
        return jnp.dot(attended, out_weight, preferred_element_type=jnp.float32).astype(jnp.bfloat16)

    outputs = lax.map(one_block, jnp.arange(block_count, dtype=jnp.int32))
    return outputs.reshape(TOKENS, HEADS * HEAD)
```

```python
import functools

import jax
import jax.numpy as jnp
from jax import lax
from jax.experimental import pallas as pl
from jax.experimental.pallas import tpu as pltpu
from jax.sharding import PartitionSpec as P

HEADS = 8
HEAD = 128
LOCAL_BITS = 10
TOK = 1024
TILE = 256
ITEMS = 8
ROWS = 64
MESH = pl.DeviceIdType.MESH
F32 = jnp.float32
BF16 = jnp.bfloat16

AT_C = 1
AT_X = 4
AT_Y = 7
AT_F1 = 9
AT_Z1 = 9
AT_Z2 = 11
AT_Z3 = 13
AT_F2 = 14
AT_L = 2
AT_R = 11
STEPS = ITEMS + AT_F2


def nt(a, b):
    return lax.dot_general(a, b, (((1,), (1,)), ((), ())), preferred_element_type=F32)


def nn(a, b):
    return jnp.dot(a, b, preferred_element_type=F32)


def bit_length(values, bits):
    count = jnp.zeros(values.shape, jnp.int32)
    for shift in range(bits):
        count = count + (jnp.right_shift(values, shift) > 0).astype(jnp.int32)
    return count


def diagonal_mixing(lam):
    group = lax.broadcasted_iota(jnp.int32, (16, 128), 0)
    token16 = lax.broadcasted_iota(jnp.int32, (16, 128), 1)
    far = bit_length(jnp.bitwise_xor(group, jnp.right_shift(token16, 3)), 4)
    coarse = jnp.where(far == 1, lam[4], jnp.where(far == 2, lam[5], jnp.where(far == 3, lam[6], lam[7])))
    coarse = jnp.where(group < jnp.right_shift(token16, 3), coarse, 0.0)
    row = lax.broadcasted_iota(jnp.int32, (8, 128), 0)
    token8 = jnp.bitwise_and(lax.broadcasted_iota(jnp.int32, (8, 128), 1), 7)
    near = bit_length(jnp.bitwise_xor(row, token8), 3)
    fine = jnp.where(near == 0, lam[0], jnp.where(near == 1, lam[1], jnp.where(near == 2, lam[2], lam[3])))
    fine = jnp.where(row <= token8, fine, 0.0)
    major = lax.broadcasted_iota(jnp.int32, (16, 8, 128), 0)
    token = lax.broadcasted_iota(jnp.int32, (16, 8, 128), 2)
    spread = jnp.broadcast_to(coarse[:, None, :], (16, 8, 128))
    return jnp.where(jnp.right_shift(token, 3) == major, fine[None], spread).reshape(128, 128)


def kernel(
    q_hbm, k_hbm, v_hbm, lam_hbm, out_hbm,
    qv, kv, vv, lamv, vt, st, ps, xb, sx, yb, sy, zo, z1b, z2b, z3b, p_out, q_out, fwd, bk, lst, acc, att,
    load_sem, core_s, core_r, x_s, x_r, y_s, y_r, z1_s, z1_r, z2_s, z2_r, z3_s, z3_r, f_s, f_r, out_sem,
):
    z = lax.axis_index("outer")
    inner = lax.axis_index("inner")
    c = inner % 2
    x = (inner // 2) % 4
    y = inner // 8

    def device(z_to, y_to, x_to, c_to):
        return (z_to, (y_to * 4 + x_to) * 2 + c_to)

    mate = device(z, y, x, 1 - c)

    def load(kind, h):
        cols = pl.ds(h * HEAD, HEAD)
        source, target = ((k_hbm, kv), (v_hbm, vv), (q_hbm, qv))[kind]
        return pltpu.make_async_copy(source.at[:, cols], target.at[h], load_sem.at[kind, h])

    def load_dyn(kind, h):
        target = (kv, vv, qv)[kind]
        return pltpu.make_async_copy(
            k_hbm.at[:, pl.ds(0, HEAD)], target.at[h], load_sem.at[kind, h])

    def lam_copy():
        return pltpu.make_async_copy(lam_hbm, lamv, load_sem.at[3, 0])

    for h in range(HEADS):
        load(0, h).start()
        load(1, h).start()
    lam_copy().start()
    for h in range(HEADS):
        load(2, h).start()

    barrier = pltpu.get_barrier_semaphore()
    peers = [mate]
    peers += [device(z, y, (x + d) % 4, c) for d in (1, 2, 3)]
    peers += [device(z, (y + d) % 4, x, c) for d in (1, 2, 3)]
    peers += [device((z + d) % 8, y, x, c) for d in range(1, 8)]
    for peer in peers:
        pl.semaphore_signal(barrier, inc=1, device_id=peer, device_id_type=MESH)

    def remote(src, dst, send, recv, to):
        return pltpu.make_async_remote_copy(
            src_ref=src, dst_ref=dst, send_sem=send, recv_sem=recv, device_id=to, device_id_type=MESH)

    def cp_core(h):
        return remote(st.at[h], ps.at[h], core_s.at[h], core_r.at[h], mate)

    def cp_x(i, d):
        return remote(xb.at[i, x], xb.at[i, x], x_s.at[i, d - 1], x_r.at[i, x], device(z, y, (x + d) % 4, c))

    def got_x(i, d):
        s = (x + d) % 4
        return remote(xb.at[i, s], xb.at[i, s], x_s.at[i, d - 1], x_r.at[i, s], device(z, y, s, c))

    def cp_y(i, d):
        return remote(yb.at[i, y], yb.at[i, y], y_s.at[i, d - 1], y_r.at[i, y], device(z, (y + d) % 4, x, c))

    def got_y(i, d):
        s = (y + d) % 4
        return remote(yb.at[i, s], yb.at[i, s], y_s.at[i, d - 1], y_r.at[i, s], device(z, s, x, c))

    def at_z(to):
        return device(to, y, x, c)

    z_pair = z + 1 - 2 * (z % 2)
    sends_1 = jnp.logical_or(z < 4, z % 2 == 0)
    gets_1 = jnp.logical_or(z < 4, z % 2 == 1)
    low = z % 4
    sends_2 = low == 1
    sends_2b = z == 2
    gets_2 = jnp.logical_or(low >= 2, z == 0)
    sends_3 = jnp.logical_or(z == 0, z == 3)
    gets_3 = z >= 4
    z3_a = jnp.where(z == 0, 7, 4)
    z3_b = jnp.where(z == 0, 6, 5)

    def cp_z1(i):
        return remote(zo.at[i], z1b.at[i], z1_s.at[i], z1_r.at[i], at_z(z_pair))

    def cp_z2(i, n, to):
        return remote(p_out.at[i], z2b.at[i], z2_s.at[i, n], z2_r.at[i], at_z(to))

    def cp_z3(i, n, to):
        return remote(q_out.at[i], z3b.at[i], z3_s.at[i, n], z3_r.at[i], at_z(to))

    def cp_f(src, i, n):
        return remote(src, fwd.at[i, n], f_s.at[i, n], f_r.at[i, n], mate)

    x_odd, x_high, y_odd, y_high = x % 2 == 1, x >= 2, y % 2 == 1, y >= 2
    z_odd, z_mid, z_high = z % 2 == 1, low >= 2, z >= 4
    has = (x_odd, x_high, y_odd, y_high, z_odd, z_mid, z_high)

    def fwd_source(i, n):
        return (
            lambda: xb.at[i, x - 1], lambda: sx.at[i], lambda: yb.at[i, y - 1], lambda: sy.at[i],
            lambda: z1b.at[i], lambda: z2b.at[i], lambda: z3b.at[i],
        )[n]()

    def hand_over(i, n):
        @pl.when(has[n])
        def _():
            source = fwd_source(i, n)
            cp_f(source, i, n).start()
            bk[2 * (i // 2) + c, 1 + n, i % 2] = source[...].astype(BF16)

    def take_over(i, n):
        @pl.when(has[n])
        def _():
            cp_f(fwd.at[i, n], i, n).wait_recv()
            bk[2 * (i // 2) + 1 - c, 1 + n, i % 2] = fwd[i, n].astype(BF16)

    def states(h):
        load_dyn(0, h).wait()
        load_dyn(1, h).wait()
        vt[h] = jnp.transpose(vv[h])
        part = []
        for p in range(4):
            part.append(nn(vt[h, :, p * TILE:(p + 1) * TILE], kv[h, p * TILE:(p + 1) * TILE, :]))
        first = part[0] + part[1]
        lst[h, 0] = part[0].astype(BF16)
        lst[h, 1] = part[2].astype(BF16)
        lst[h, 2] = first.astype(BF16)
        st[h] = (first + (part[2] + part[3])).reshape(2, ROWS, HEAD)

    def step_c(i):
        h = 2 * (i // 2) + c

        @pl.when(i % 2 == 0)
        def _():
            for n in range(2):
                cp_core(i + n).wait_recv()

                @pl.when(c == 1)
                def _():
                    bk[i + n, 0] = ps[i + n].astype(BF16)

        xb[i, x] = st[h, i % 2] + ps[h, i % 2]
        for d in (2, 1, 3):
            cp_x(i, d).start()

    def step_x(i):
        for d in (1, 2, 3):
            got_x(i, d).wait_recv()
        front = xb[i, 0] + xb[i, 1]
        sx[i] = front
        yb[i, y] = front + (xb[i, 2] + xb[i, 3])
        for d in (2, 1, 3):
            cp_y(i, d).start()
        hand_over(i, 0)
        hand_over(i, 1)

    def step_y(i):
        for d in (1, 2, 3):
            got_y(i, d).wait_recv()
        front = yb[i, 0] + yb[i, 1]
        sy[i] = front
        zo[i] = front + (yb[i, 2] + yb[i, 3])

        @pl.when(sends_1)
        def _():
            cp_z1(i).start()
        hand_over(i, 2)
        hand_over(i, 3)

    def step_z1(i):
        @pl.when(gets_1)
        def _():
            cp_z1(i).wait_recv()
            p_out[i] = zo[i] + z1b[i]

        @pl.when(sends_2)
        def _():
            cp_z2(i, 1, z + 2).start()
            cp_z2(i, 0, z + 1).start()

        @pl.when(sends_2b)
        def _():
            cp_z2(i, 0, 0).start()
        hand_over(i, 4)

    def step_z2(i):
        @pl.when(gets_2)
        def _():
            cp_z2(i, 0, 0).wait_recv()

        @pl.when(sends_3)
        def _():
            q_out[i] = p_out[i] + z2b[i]
            cp_z3(i, 1, z3_b).start()
            cp_z3(i, 0, z3_a).start()
        hand_over(i, 5)

    def step_z3(i):
        @pl.when(gets_3)
        def _():
            cp_z3(i, 0, 0).wait_recv()
        hand_over(i, 6)

    def local(h):
        load_dyn(2, h).wait()

        @pl.when(h == 0)
        def _():
            lam_copy().wait()
        for p in range(4):
            at = p * TILE
            qp = qv[h, at:at + TILE, :]
            kp = kv[h, at:at + TILE, :]
            scores = nt(kp, qp)
            rows = [lamv[l, pl.ds(h, 1), at:at + TILE] for l in range(LOCAL_BITS + 1)]
            mix_a = diagonal_mixing([row[:, :128] for row in rows[:8]])
            mix_b = diagonal_mixing([row[:, 128:] for row in rows[:8]])
            top = jnp.concatenate(
                [scores[:128, :128] * mix_a, scores[:128, 128:] * rows[8][:, 128:]], axis=1).astype(BF16)
            low_part = jnp.concatenate(
                [jnp.zeros((128, 128), BF16), (scores[128:, 128:] * mix_b).astype(BF16)], axis=1)
            weighted = jnp.concatenate([top, low_part], axis=0)
            total = nn(vt[h, :, at:at + TILE], weighted)
            if p % 2 == 1:
                total = total + rows[9] * nt(lst[h, p // 2], qp)
            if p >= 2:
                total = total + rows[10] * nt(lst[h, 2], qp)
            acc[h, :, at:at + TILE] = total

    def distant(h, first, last, done):
        count = last - first
        for p in range(4):
            at = p * TILE
            qp = qv[h, at:at + TILE, :]
            products = nt(bk[h, first:last].reshape(count * HEAD, HEAD), qp)
            total = acc[h, :, at:at + TILE]
            for n in range(count):
                row = lamv[LOCAL_BITS + 1 + first + n, pl.ds(h, 1), at:at + TILE]
                total = total + products[n * HEAD:(n + 1) * HEAD] * row
            if done:
                att[h, :, at:at + TILE] = total.astype(BF16)
            else:
                acc[h, :, at:at + TILE] = total

    def out_copy(h):
        return pltpu.make_async_copy(
            att.at[h], out_hbm.at[pl.ds(pl.multiple_of(h * HEAD, HEAD), HEAD), :], out_sem.at[h])

    def when_in(t, at, count):
        return jnp.logical_and(t >= at, t < at + count)

    def step(t, carry):
        def stage(at, run, count=ITEMS):
            @pl.when(when_in(t, at, count))
            def _():
                run(t - at)

        stage(AT_Z3, step_z3)
        stage(AT_Z2, step_z2)
        stage(AT_Z1, step_z1)
        stage(AT_Y, step_y)
        stage(AT_X, step_x)
        stage(AT_C, step_c)

        @pl.when(jnp.logical_and(jnp.logical_and(t % 2 == 0, t > 0), t < ITEMS))
        def _():
            for n in range(2):
                states(t + n)
                cp_core(t + n).start()

        stage(AT_L, local)

        def f1(i):
            for n in range(4):
                take_over(i, n)
        stage(AT_F1, f1)
        stage(AT_R, lambda h: distant(h, 0, 5, False))

        def f2(i):
            for n in range(4, 7):
                take_over(i, n)

            @pl.when(i % 2 == 1)
            def _():
                for n in range(2):
                    distant(i - 1 + n, 5, 8, True)
                    out_copy(i - 1 + n).start()
        stage(AT_F2, f2)
        return carry

    bk[...] = jnp.zeros(bk.shape, BF16)
    states(0)
    states(1)
    pl.semaphore_wait(barrier, len(peers))
    cp_core(0).start()
    cp_core(1).start()
    lax.fori_loop(1, STEPS, step, 0)

    def drain(i, carry):
        cp_core(i).wait_send()
        for d in (1, 2, 3):
            cp_x(i, d).wait_send()
            cp_y(i, d).wait_send()

        @pl.when(sends_1)
        def _():
            cp_z1(i).wait_send()

        @pl.when(jnp.logical_or(sends_2, sends_2b))
        def _():
            cp_z2(i, 0, 0).wait_send()

        @pl.when(sends_2)
        def _():
            cp_z2(i, 1, 0).wait_send()

        @pl.when(sends_3)
        def _():
            cp_z3(i, 0, 0).wait_send()
            cp_z3(i, 1, 0).wait_send()
        for n in range(7):
            @pl.when(has[n])
            def _():
                cp_f(fwd.at[i, n], i, n).wait_send()
        out_copy(i).wait()
        return carry

    lax.fori_loop(0, ITEMS, drain, 0)


def attend(queries, keys, values, level_weights):
    item = (ROWS, HEAD)
    dma = pltpu.SemaphoreType.DMA
    scratch = [
        pltpu.VMEM((HEADS, TOK, HEAD), BF16),
        pltpu.VMEM((HEADS, TOK, HEAD), BF16),
        pltpu.VMEM((HEADS, TOK, HEAD), BF16),
        pltpu.VMEM(level_weights.shape, F32),
        pltpu.VMEM((HEADS, HEAD, TOK), BF16),
        pltpu.VMEM((HEADS, 2) + item, F32),
        pltpu.VMEM((HEADS, 2) + item, F32),
        pltpu.VMEM((ITEMS, 4) + item, F32),
        pltpu.VMEM((ITEMS,) + item, F32),
        pltpu.VMEM((ITEMS, 4) + item, F32),
        pltpu.VMEM((ITEMS,) + item, F32),
        pltpu.VMEM((ITEMS,) + item, F32),
        pltpu.VMEM((ITEMS,) + item, F32),
        pltpu.VMEM((ITEMS,) + item, F32),
        pltpu.VMEM((ITEMS,) + item, F32),
        pltpu.VMEM((ITEMS,) + item, F32),
        pltpu.VMEM((ITEMS,) + item, F32),
        pltpu.VMEM((ITEMS, 7) + item, F32),
        pltpu.VMEM((HEADS, 8, 2) + item, BF16),
        pltpu.VMEM((HEADS, 3, HEAD, HEAD), BF16),
        pltpu.VMEM((HEADS, HEAD, TOK), F32),
        pltpu.VMEM((HEADS, HEAD, TOK), BF16),
        dma((4, HEADS)),
        dma((HEADS,)), dma((HEADS,)),
        dma((ITEMS, 3)), dma((ITEMS, 4)),
        dma((ITEMS, 3)), dma((ITEMS, 4)),
        dma((ITEMS,)), dma((ITEMS,)),
        dma((ITEMS, 2)), dma((ITEMS,)),
        dma((ITEMS, 2)), dma((ITEMS,)),
        dma((ITEMS, 7)), dma((ITEMS, 7)),
        dma((HEADS,)),
    ]
    return pl.pallas_call(
        kernel,
        out_shape=jax.ShapeDtypeStruct((HEADS * HEAD, TOK), BF16),
        in_specs=[pl.BlockSpec(memory_space=pl.ANY)] * 4,
        out_specs=pl.BlockSpec(memory_space=pl.ANY),
        scratch_shapes=scratch,
        compiler_params=pltpu.CompilerParams(
            collective_id=0, has_side_effects=True, vmem_limit_bytes=60 << 20),
    )(queries, keys, values, level_weights)


def body(queries, keys, values, level_weights, out_weight):
    attended = attend(queries, keys, values, level_weights)
    return lax.dot_general(
        attended, out_weight, (((0,), (0,)), ((), ())), preferred_element_type=F32).astype(BF16)


def solution(mesh):
    rows = P(("outer", "inner"), None)
    in_specs = (rows, rows, rows, P(None, None, ("outer", "inner")), P())
    return jax.shard_map(body, mesh=mesh, in_specs=in_specs, out_specs=rows, check_vma=False)
```

```python
import jax
import jax.numpy as jnp
from jax import lax
from jax.experimental import pallas as pl
from jax.experimental.pallas import tpu as pltpu
from jax.sharding import PartitionSpec as P

HEADS = 8
HEAD = 128
LOCAL_BITS = 10
TOK = 1024
TILE = 256
VMEM_MIB = 50
PARTS = 2
ITEMS = 4 * PARTS
ROWS = HEAD // PARTS
STRIDE = PARTS // 2
MESH = pl.DeviceIdType.MESH
F32 = jnp.float32
BF16 = jnp.bfloat16

AT_C = 1
AT_X = 4
AT_Y = 7
AT_F1 = 9
AT_Z1 = 9
AT_Z2 = 12
AT_Z3 = 15
AT_F2 = 16
AT_L = 3
AT_R = 13
STEPS = ITEMS + AT_F2


def nt(a, b):
    return lax.dot_general(a, b, (((1,), (1,)), ((), ())), preferred_element_type=F32)


def nn(a, b):
    return jnp.dot(a, b, preferred_element_type=F32)


def bit_length(values, bits):
    count = jnp.zeros(values.shape, jnp.int32)
    for shift in range(bits):
        count = count + (jnp.right_shift(values, shift) > 0).astype(jnp.int32)
    return count


def diagonal_mixing(lam):
    group = lax.broadcasted_iota(jnp.int32, (16, 128), 0)
    token16 = lax.broadcasted_iota(jnp.int32, (16, 128), 1)
    far = bit_length(jnp.bitwise_xor(group, jnp.right_shift(token16, 3)), 4)
    coarse = jnp.where(far == 1, lam[4], jnp.where(far == 2, lam[5], jnp.where(far == 3, lam[6], lam[7])))
    coarse = jnp.where(group < jnp.right_shift(token16, 3), coarse, 0.0)
    row = lax.broadcasted_iota(jnp.int32, (8, 128), 0)
    token8 = jnp.bitwise_and(lax.broadcasted_iota(jnp.int32, (8, 128), 1), 7)
    near = bit_length(jnp.bitwise_xor(row, token8), 3)
    fine = jnp.where(near == 0, lam[0], jnp.where(near == 1, lam[1], jnp.where(near == 2, lam[2], lam[3])))
    fine = jnp.where(row <= token8, fine, 0.0)
    major = lax.broadcasted_iota(jnp.int32, (16, 8, 128), 0)
    token = lax.broadcasted_iota(jnp.int32, (16, 8, 128), 2)
    spread = jnp.broadcast_to(coarse[:, None, :], (16, 8, 128))
    return jnp.where(jnp.right_shift(token, 3) == major, fine[None], spread).reshape(128, 128)


def kernel(
    q_hbm, k_hbm, v_hbm, lam_hbm, out_hbm,
    qv, kv, vv, lamv, vt, st, ps, xb, sx, yb, sy, zo, zr, p_out, q_out, fwd, bk, lst, acc, att_t, att,
    load_sem, whole_sem, core_s, core_r, x_s, x_r, y_s, y_r, z_s, z_r, f_s, f_r, out_sem,
):
    z = lax.axis_index("outer")
    inner = lax.axis_index("inner")
    c = inner % 2
    x = (inner // 2) % 4
    y = inner // 8

    def device(z_to, y_to, x_to, c_to):
        return (z_to, (y_to * 4 + x_to) * 2 + c_to)

    mate = device(z, y, x, 1 - c)

    def load(kind, h, source_h):
        source, target = ((k_hbm, kv), (v_hbm, vv), (q_hbm, qv))[kind]
        return pltpu.make_async_copy(
            source.at[:, pl.ds(source_h * HEAD, HEAD)], target.at[h], load_sem.at[kind, h])

    lam_copy = pltpu.make_async_copy(lam_hbm, lamv, whole_sem.at[0])

    for h in range(HEADS):
        load(0, h, h).start()
        load(1, h, h).start()
    lam_copy.start()
    for h in range(HEADS):
        load(2, h, h).start()

    barrier = pltpu.get_barrier_semaphore()
    peers = [mate]
    peers += [device(z, y, (x + d) % 4, c) for d in (1, 2, 3)]
    peers += [device(z, (y + d) % 4, x, c) for d in (1, 2, 3)]
    peers += [device((z + d) % 8, y, x, c) for d in (1, 7, 2, 6)]
    for peer in peers:
        pl.semaphore_signal(barrier, inc=1, device_id=peer, device_id_type=MESH)

    def remote(src, dst, send, recv, to):
        return pltpu.make_async_remote_copy(
            src_ref=src, dst_ref=dst, send_sem=send, recv_sem=recv, device_id=to, device_id_type=MESH)

    def at_x(d):
        return device(z, y, (x + d) % 4, c)

    def at_y(d):
        return device(z, (y + d) % 4, x, c)

    def at_z(to):
        return device(to, y, x, c)

    def cp_core(h):
        return remote(st.at[h], ps.at[h], core_s.at[0], core_r.at[h // 2], mate)

    def got_core(k):
        pair = ps.at[pl.ds(2 * k, 2)]
        return remote(pair, pair, core_s.at[0], core_r.at[k], mate)

    def cp_x(i, d):
        return remote(xb.at[i, x], xb.at[i, x], x_s.at[0], x_r.at[i], at_x(d))

    def got_x(i):
        return remote(xb.at[i, pl.ds(0, 3)], xb.at[i, pl.ds(0, 3)], x_s.at[0], x_r.at[i], at_x(1))

    def cp_y(i, d):
        return remote(yb.at[i, y], yb.at[i, y], y_s.at[0], y_r.at[i], at_y(d))

    def got_y(i):
        return remote(yb.at[i, pl.ds(0, 3)], yb.at[i, pl.ds(0, 3)], y_s.at[0], y_r.at[i], at_y(1))

    x_pair = x + 1 - 2 * (x % 2)
    y_pair = y + 1 - 2 * (y % 2)
    z_pair = z + 1 - 2 * (z % 2)
    low = z % 4
    sends_1 = jnp.logical_or(z < 4, z % 2 == 0)
    gets_1 = jnp.logical_or(z < 4, z % 2 == 1)
    sends_2 = low == 1
    sends_2b = z == 2
    gets_2 = jnp.logical_or(low >= 2, z == 0)
    sends_3 = jnp.logical_or(z == 0, z == 3)
    gets_3 = z >= 4
    z3_a = jnp.where(z == 0, 7, 4)
    z3_b = jnp.where(z == 0, 6, 5)

    def cp_z(n, source, i, to):
        return remote(source.at[i], zr.at[i, n], z_s.at[n], z_r.at[i, n], at_z(to))

    def got_z(n, i):
        return remote(zr.at[i, n], zr.at[i, n], z_s.at[n], z_r.at[i, n], at_z(z_pair))

    def sent_z(n, source):
        return remote(source, source, z_s.at[n], z_r.at[0, n], at_z(z_pair))

    has = (x % 2 == 1, x >= 2, y % 2 == 1, y >= 2, z % 2 == 1, low >= 2, z >= 4)
    places = ((0, 2), (2, 2), (4, 3))

    def cp_f(source, i, kind):
        first, count = places[kind]
        return remote(source.at[i], fwd.at[i, pl.ds(first, count)], f_s.at[0], f_r.at[i, kind], mate)

    def keep(h, i, n, value):
        bk[h, 1 + n, i % PARTS] = jnp.where(has[n], value, 0.0).astype(BF16)

    def hand_over(source, i, kind):
        cp_f(source, i, kind).start()
        first, count = places[kind]
        for n in range(count):
            keep(2 * (i // PARTS) + c, i, first + n, source[i, n])

    def take_over(i, kind):
        first, count = places[kind]
        there = fwd.at[i, pl.ds(first, count)]
        remote(there, there, f_s.at[0], f_r.at[i, kind], mate).wait_recv()
        for n in range(count):
            keep(2 * (i // PARTS) + 1 - c, i, first + n, fwd[i, first + n])

    def states(h):
        load(0, h, 0).wait()
        load(1, h, 0).wait()
        vt[h] = jnp.transpose(vv[h])
        part = []
        for p in range(4):
            part.append(nn(vt[h, :, p * TILE:(p + 1) * TILE], kv[h, p * TILE:(p + 1) * TILE, :]))
        first = part[0] + part[1]
        lst[h, 0] = part[0].astype(BF16)
        lst[h, 1] = part[2].astype(BF16)
        lst[h, 2] = first.astype(BF16)
        st[h] = (first + (part[2] + part[3])).reshape(PARTS, ROWS, HEAD)

    def step_c(i):
        h = 2 * (i // PARTS) + c

        @pl.when(i % PARTS == 0)
        def _():
            got_core(i // PARTS).wait_recv()
            for n in range(2):
                g = 2 * (i // PARTS) + n
                bk[g, 0] = jnp.where(c == 1, ps[g], 0.0).astype(BF16)

        xb[i, x] = st[h, i % PARTS] + ps[h, i % PARTS]
        for d in (2, 1, 3):
            cp_x(i, d).start()

    def step_x(i):
        got_x(i).wait_recv()
        front = xb[i, 0] + xb[i, 1]
        yb[i, y] = front + (xb[i, 2] + xb[i, 3])
        for d in (2, 1, 3):
            cp_y(i, d).start()
        sx[i, 0] = xb[i, x_pair]
        sx[i, 1] = front
        hand_over(sx, i, 0)

    def step_y(i):
        got_y(i).wait_recv()
        front = yb[i, 0] + yb[i, 1]
        zo[i] = front + (yb[i, 2] + yb[i, 3])

        @pl.when(sends_1)
        def _():
            cp_z(0, zo, i, z_pair).start()
        sy[i, 0] = yb[i, y_pair]
        sy[i, 1] = front
        hand_over(sy, i, 1)

    def step_z1(i):
        @pl.when(gets_1)
        def _():
            got_z(0, i).wait_recv()
            p_out[i] = zo[i] + zr[i, 0]

        @pl.when(sends_2)
        def _():
            cp_z(1, p_out, i, z + 2).start()
            cp_z(1, p_out, i, z + 1).start()

        @pl.when(sends_2b)
        def _():
            cp_z(1, p_out, i, 0).start()

    def step_z2(i):
        @pl.when(gets_2)
        def _():
            got_z(1, i).wait_recv()

        @pl.when(sends_3)
        def _():
            q_out[i] = p_out[i] + zr[i, 1]
            cp_z(2, q_out, i, z3_b).start()
            cp_z(2, q_out, i, z3_a).start()

    def step_z3(i):
        @pl.when(gets_3)
        def _():
            got_z(2, i).wait_recv()
        hand_over(zr, i, 2)

    def local(h):
        load(2, h, 0).wait()

        @pl.when(h == 0)
        def _():
            lam_copy.wait()
        for p in range(4):
            at = p * TILE
            qp = qv[h, at:at + TILE, :]
            kp = kv[h, at:at + TILE, :]
            scores = nt(kp, qp)
            rows = [lamv[l, pl.ds(h, 1), at:at + TILE] for l in range(LOCAL_BITS + 1)]
            mix_a = diagonal_mixing([row[:, :128] for row in rows[:8]])
            mix_b = diagonal_mixing([row[:, 128:] for row in rows[:8]])
            top = jnp.concatenate(
                [scores[:128, :128] * mix_a, scores[:128, 128:] * rows[8][:, 128:]], axis=1).astype(BF16)
            low_part = jnp.concatenate(
                [jnp.zeros((128, 128), BF16), (scores[128:, 128:] * mix_b).astype(BF16)], axis=1)
            weighted = jnp.concatenate([top, low_part], axis=0)
            total = nn(vt[h, :, at:at + TILE], weighted)
            if p % 2 == 1:
                total = total + rows[9] * nt(lst[h, p // 2], qp)
            if p >= 2:
                total = total + rows[10] * nt(lst[h, 2], qp)
            acc[h, :, :, at:at + TILE] = total.reshape(PARTS, ROWS, TILE)

    def distant(states_there, h, p, first, total):
        at = p * TILE
        rows = total.shape[0]
        products = nt(states_there, qv[h, at:at + TILE, :])
        for n in range(states_there.shape[0] // rows):
            row = lamv[LOCAL_BITS + 1 + first + n, pl.ds(h, 1), at:at + TILE]
            total = total + products[n * rows:(n + 1) * rows] * row
        return total

    def near_buckets(h):
        for p in range(4):
            at = p * TILE
            total = distant(bk[h, 0:5].reshape(5 * HEAD, HEAD), h, p, 0, acc[h, :, :, at:at + TILE].reshape(HEAD, TILE))
            acc[h, :, :, at:at + TILE] = total.reshape(PARTS, ROWS, TILE)

    def out_copy(h):
        return pltpu.make_async_copy(
            att.at[h], out_hbm.at[:, pl.ds(pl.multiple_of(h * HEAD, HEAD), HEAD)], out_sem.at[h])

    def far_buckets(i):
        part = i % PARTS
        for n in range(2):
            h = 2 * (i // PARTS) + n
            for p in range(4):
                at = p * TILE
                total = distant(bk[h, 5:8, part].reshape(3 * ROWS, HEAD), h, p, 5, acc[h, part, :, at:at + TILE])
                att_t[h, part, :, at:at + TILE] = total.astype(BF16)

        @pl.when(part == PARTS - 1)
        def _():
            for n in range(2):
                h = 2 * (i // PARTS) + n
                att[h] = jnp.transpose(att_t[h].reshape(HEAD, TOK))
                out_copy(h).start()

    def when_in(t, at, count):
        return jnp.logical_and(t >= at, t < at + count)

    def step(t, carry):
        def stage(at, run, count=ITEMS):
            @pl.when(when_in(t, at, count))
            def _():
                run(t - at)

        def spread(at, run):
            @pl.when(jnp.logical_and(when_in(t, at, HEADS * STRIDE), (t - at) % STRIDE == 0))
            def _():
                run((t - at) // STRIDE)

        def f1(i):
            take_over(i, 0)
            take_over(i, 1)

        def f2(i):
            take_over(i, 2)
            far_buckets(i)

        stage(AT_X, step_x)
        stage(AT_Z3, step_z3)
        stage(AT_Z2, step_z2)
        stage(AT_Y, step_y)
        stage(AT_Z1, step_z1)
        stage(AT_C, step_c)

        @pl.when(jnp.logical_and(t % PARTS == 0, t < ITEMS))
        def _():
            for n in range(2):
                g = 2 * (t // PARTS) + n
                states(g)
                cp_core(g).start()

        stage(AT_F1, f1)
        stage(AT_F2, f2)
        early = jnp.logical_and(jnp.logical_and(t >= AT_L, t < AT_L + 6), (t - AT_L) % 2 == 0)
        late = when_in(t, AT_L + 5, HEADS - 3)

        @pl.when(jnp.logical_or(early, late))
        def _():
            local(jnp.where(early, (t - AT_L) // 2, t - AT_L - 2))
        spread(AT_R, near_buckets)
        return carry

    states(0)
    states(1)
    pl.semaphore_wait(barrier, len(peers))
    cp_core(0).start()
    cp_core(1).start()
    lax.fori_loop(1, STEPS, step, 0)

    remote(st, st, core_s.at[0], core_r.at[0], mate).wait_send()
    remote(xb.at[:, pl.ds(0, 3)], xb.at[:, pl.ds(0, 3)], x_s.at[0], x_r.at[0], at_x(1)).wait_send()
    remote(yb.at[:, pl.ds(0, 3)], yb.at[:, pl.ds(0, 3)], y_s.at[0], y_r.at[0], at_y(1)).wait_send()

    @pl.when(sends_1)
    def _():
        sent_z(0, zo).wait_send()

    @pl.when(sends_2)
    def _():
        sent_z(1, sx).wait_send()

    @pl.when(sends_2b)
    def _():
        sent_z(1, zo).wait_send()

    @pl.when(sends_3)
    def _():
        sent_z(2, sx).wait_send()
    remote(fwd, fwd, f_s.at[0], f_r.at[0, 0], mate).wait_send()
    for h in range(HEADS):
        out_copy(h).wait()


def layer(queries, keys, values, level_weights, out_weight):
    item = (ROWS, HEAD)
    dma = pltpu.SemaphoreType.DMA
    scratch = [
        pltpu.VMEM((HEADS, TOK, HEAD), BF16),
        pltpu.VMEM((HEADS, TOK, HEAD), BF16),
        pltpu.VMEM((HEADS, TOK, HEAD), BF16),
        pltpu.VMEM(level_weights.shape, F32),
        pltpu.VMEM((HEADS, HEAD, TOK), BF16),
        pltpu.VMEM((HEADS, PARTS) + item, F32),
        pltpu.VMEM((HEADS, PARTS) + item, F32),
        pltpu.VMEM((ITEMS, 4) + item, F32),
        pltpu.VMEM((ITEMS, 2) + item, F32),
        pltpu.VMEM((ITEMS, 4) + item, F32),
        pltpu.VMEM((ITEMS, 2) + item, F32),
        pltpu.VMEM((ITEMS,) + item, F32),
        pltpu.VMEM((ITEMS, 3) + item, F32),
        pltpu.VMEM((ITEMS,) + item, F32),
        pltpu.VMEM((ITEMS,) + item, F32),
        pltpu.VMEM((ITEMS, 7) + item, F32),
        pltpu.VMEM((HEADS, 8, PARTS) + item, BF16),
        pltpu.VMEM((HEADS, 3, HEAD, HEAD), BF16),
        pltpu.VMEM((HEADS, PARTS, ROWS, TOK), F32),
        pltpu.VMEM((HEADS, PARTS, ROWS, TOK), BF16),
        pltpu.VMEM((HEADS, TOK, HEAD), BF16),
        dma((3, HEADS)), dma((1,)),
        dma((1,)), dma((HEADS // 2,)),
        dma((1,)), dma((ITEMS,)),
        dma((1,)), dma((ITEMS,)),
        dma((3,)), dma((ITEMS, 3)),
        dma((1,)), dma((ITEMS, 3)),
        dma((HEADS,)),
    ]
    attended = pl.pallas_call(
        kernel,
        out_shape=jax.ShapeDtypeStruct((TOK, HEADS * HEAD), BF16),
        in_specs=[pl.BlockSpec(memory_space=pl.ANY)] * 4,
        out_specs=pl.BlockSpec(memory_space=pl.ANY),
        scratch_shapes=scratch,
        compiler_params=pltpu.CompilerParams(
            collective_id=0, has_side_effects=True, vmem_limit_bytes=VMEM_MIB << 20),
    )(*[pltpu.with_memory_space_constraint(a, pltpu.HBM) for a in (queries, keys, values, level_weights)])
    return jnp.dot(attended, out_weight, preferred_element_type=F32).astype(BF16)


def solution(mesh):
    rows = P(("outer", "inner"), None)
    in_specs = (rows, rows, rows, P(None, None, ("outer", "inner")), P())
    return jax.shard_map(layer, mesh=mesh, in_specs=in_specs, out_specs=rows, check_vma=False)
```

```python
import jax
import jax.numpy as jnp
from jax import lax
from jax.experimental import pallas as pl
from jax.experimental.pallas import tpu as pltpu
from jax.sharding import PartitionSpec as P

HEADS = 8
HEAD = 128
LOCAL_BITS = 10
TOK = 1024
TILE = 256
VMEM_MIB = 50
PARTS = 2
ITEMS = 4 * PARTS
ROWS = HEAD // PARTS
STRIDE = PARTS // 2
MESH = pl.DeviceIdType.MESH
F32 = jnp.float32
BF16 = jnp.bfloat16

AT_C = 1
AT_X = 4
AT_Y = 7
AT_F1 = 9
AT_Z1 = 9
AT_Z2 = 12
AT_Z3 = 15
AT_F2 = 16
AT_L = 3
AT_R = 13
STEPS = ITEMS + AT_F2


def nt(a, b):
    return lax.dot_general(a, b, (((1,), (1,)), ((), ())), preferred_element_type=F32)


def nn(a, b):
    return jnp.dot(a, b, preferred_element_type=F32)


def bit_length(values, bits):
    count = jnp.zeros(values.shape, jnp.int32)
    for shift in range(bits):
        count = count + (jnp.right_shift(values, shift) > 0).astype(jnp.int32)
    return count


def diagonal_mixing(lam):
    group = lax.broadcasted_iota(jnp.int32, (16, 128), 0)
    token16 = lax.broadcasted_iota(jnp.int32, (16, 128), 1)
    far = bit_length(jnp.bitwise_xor(group, jnp.right_shift(token16, 3)), 4)
    coarse = jnp.where(far == 1, lam[4], jnp.where(far == 2, lam[5], jnp.where(far == 3, lam[6], lam[7])))
    coarse = jnp.where(group < jnp.right_shift(token16, 3), coarse, 0.0)
    row = lax.broadcasted_iota(jnp.int32, (8, 128), 0)
    token8 = jnp.bitwise_and(lax.broadcasted_iota(jnp.int32, (8, 128), 1), 7)
    near = bit_length(jnp.bitwise_xor(row, token8), 3)
    fine = jnp.where(near == 0, lam[0], jnp.where(near == 1, lam[1], jnp.where(near == 2, lam[2], lam[3])))
    fine = jnp.where(row <= token8, fine, 0.0)
    major = lax.broadcasted_iota(jnp.int32, (16, 8, 128), 0)
    token = lax.broadcasted_iota(jnp.int32, (16, 8, 128), 2)
    spread = jnp.broadcast_to(coarse[:, None, :], (16, 8, 128))
    return jnp.where(jnp.right_shift(token, 3) == major, fine[None], spread).reshape(128, 128)


def kernel(
    q_hbm, k_hbm, v_hbm, lam_hbm, out,
    qv, kv, vv, lamv, vt, st, ps, xb, sx, yb, sy, zo, zr, p_out, q_out, fwd, bk, lst, acc,
    load_sem, whole_sem, core_s, core_r, x_s, x_r, y_s, y_r, z_s, z_r, f_s, f_r,
):
    z = lax.axis_index("outer")
    inner = lax.axis_index("inner")
    c = inner % 2
    x = (inner // 2) % 4
    y = inner // 8

    def device(z_to, y_to, x_to, c_to):
        return (z_to, (y_to * 4 + x_to) * 2 + c_to)

    mate = device(z, y, x, 1 - c)

    def load(kind, h, source_h):
        source, target = ((k_hbm, kv), (v_hbm, vv), (q_hbm, qv))[kind]
        return pltpu.make_async_copy(
            source.at[:, pl.ds(source_h * HEAD, HEAD)], target.at[h], load_sem.at[kind, h])

    lam_copy = pltpu.make_async_copy(lam_hbm, lamv, whole_sem.at[0])

    for h in range(HEADS):
        load(0, h, h).start()
        load(1, h, h).start()
    lam_copy.start()
    for h in range(HEADS):
        load(2, h, h).start()

    barrier = pltpu.get_barrier_semaphore()
    peers = [mate]
    peers += [device(z, y, (x + d) % 4, c) for d in (1, 2, 3)]
    peers += [device(z, (y + d) % 4, x, c) for d in (1, 2, 3)]
    peers += [device((z + d) % 8, y, x, c) for d in (1, 7, 2, 6)]
    for peer in peers:
        pl.semaphore_signal(barrier, inc=1, device_id=peer, device_id_type=MESH)

    def remote(src, dst, send, recv, to):
        return pltpu.make_async_remote_copy(
            src_ref=src, dst_ref=dst, send_sem=send, recv_sem=recv, device_id=to, device_id_type=MESH)

    def at_x(d):
        return device(z, y, (x + d) % 4, c)

    def at_y(d):
        return device(z, (y + d) % 4, x, c)

    def at_z(to):
        return device(to, y, x, c)

    def cp_core(h):
        return remote(st.at[h], ps.at[h], core_s.at[0], core_r.at[h // 2], mate)

    def got_core(k):
        pair = ps.at[pl.ds(2 * k, 2)]
        return remote(pair, pair, core_s.at[0], core_r.at[k], mate)

    def cp_x(i, d):
        return remote(xb.at[i, x], xb.at[i, x], x_s.at[0], x_r.at[i], at_x(d))

    def got_x(i):
        return remote(xb.at[i, pl.ds(0, 3)], xb.at[i, pl.ds(0, 3)], x_s.at[0], x_r.at[i], at_x(1))

    def cp_y(i, d):
        return remote(yb.at[i, y], yb.at[i, y], y_s.at[0], y_r.at[i], at_y(d))

    def got_y(i):
        return remote(yb.at[i, pl.ds(0, 3)], yb.at[i, pl.ds(0, 3)], y_s.at[0], y_r.at[i], at_y(1))

    x_pair = x + 1 - 2 * (x % 2)
    y_pair = y + 1 - 2 * (y % 2)
    z_pair = z + 1 - 2 * (z % 2)
    low = z % 4
    sends_1 = jnp.logical_or(z < 4, z % 2 == 0)
    gets_1 = jnp.logical_or(z < 4, z % 2 == 1)
    sends_2 = low == 1
    sends_2b = z == 2
    gets_2 = jnp.logical_or(low >= 2, z == 0)
    sends_3 = jnp.logical_or(z == 0, z == 3)
    gets_3 = z >= 4
    z3_a = jnp.where(z == 0, 7, 4)
    z3_b = jnp.where(z == 0, 6, 5)

    def cp_z(n, source, i, to):
        return remote(source.at[i], zr.at[i, n], z_s.at[n], z_r.at[i, n], at_z(to))

    def got_z(n, i):
        return remote(zr.at[i, n], zr.at[i, n], z_s.at[n], z_r.at[i, n], at_z(z_pair))

    def sent_z(n, source):
        return remote(source, source, z_s.at[n], z_r.at[0, n], at_z(z_pair))

    has = (x % 2 == 1, x >= 2, y % 2 == 1, y >= 2, z % 2 == 1, low >= 2, z >= 4)
    places = ((0, 2), (2, 2), (4, 3))

    def cp_f(source, i, kind):
        first, count = places[kind]
        return remote(source.at[i], fwd.at[i, pl.ds(first, count)], f_s.at[0], f_r.at[i, kind], mate)

    def keep(h, i, n, value):
        bk[h, 1 + n, i % PARTS] = jnp.where(has[n], value, 0.0).astype(BF16)

    def hand_over(source, i, kind):
        cp_f(source, i, kind).start()
        first, count = places[kind]
        for n in range(count):
            keep(2 * (i // PARTS) + c, i, first + n, source[i, n])

    def take_over(i, kind):
        first, count = places[kind]
        there = fwd.at[i, pl.ds(first, count)]
        remote(there, there, f_s.at[0], f_r.at[i, kind], mate).wait_recv()
        for n in range(count):
            keep(2 * (i // PARTS) + 1 - c, i, first + n, fwd[i, first + n])

    def states(h):
        load(0, h, 0).wait()
        load(1, h, 0).wait()
        vt[h] = jnp.transpose(vv[h])
        part = []
        for p in range(4):
            part.append(nn(vt[h, :, p * TILE:(p + 1) * TILE], kv[h, p * TILE:(p + 1) * TILE, :]))
        first = part[0] + part[1]
        lst[h, 0] = part[0].astype(BF16)
        lst[h, 1] = part[2].astype(BF16)
        lst[h, 2] = first.astype(BF16)
        st[h] = (first + (part[2] + part[3])).reshape(PARTS, ROWS, HEAD)

    def step_c(i):
        h = 2 * (i // PARTS) + c

        @pl.when(i % PARTS == 0)
        def _():
            got_core(i // PARTS).wait_recv()
            for n in range(2):
                g = 2 * (i // PARTS) + n
                bk[g, 0] = jnp.where(c == 1, ps[g], 0.0).astype(BF16)

        xb[i, x] = st[h, i % PARTS] + ps[h, i % PARTS]
        for d in (2, 1, 3):
            cp_x(i, d).start()

    def step_x(i):
        got_x(i).wait_recv()
        front = xb[i, 0] + xb[i, 1]
        yb[i, y] = front + (xb[i, 2] + xb[i, 3])
        for d in (2, 1, 3):
            cp_y(i, d).start()
        sx[i, 0] = xb[i, x_pair]
        sx[i, 1] = front
        hand_over(sx, i, 0)

    def step_y(i):
        got_y(i).wait_recv()
        front = yb[i, 0] + yb[i, 1]
        zo[i] = front + (yb[i, 2] + yb[i, 3])

        @pl.when(sends_1)
        def _():
            cp_z(0, zo, i, z_pair).start()
        sy[i, 0] = yb[i, y_pair]
        sy[i, 1] = front
        hand_over(sy, i, 1)

    def step_z1(i):
        @pl.when(gets_1)
        def _():
            got_z(0, i).wait_recv()
            p_out[i] = zo[i] + zr[i, 0]

        @pl.when(sends_2)
        def _():
            cp_z(1, p_out, i, z + 2).start()
            cp_z(1, p_out, i, z + 1).start()

        @pl.when(sends_2b)
        def _():
            cp_z(1, p_out, i, 0).start()

    def step_z2(i):
        @pl.when(gets_2)
        def _():
            got_z(1, i).wait_recv()

        @pl.when(sends_3)
        def _():
            q_out[i] = p_out[i] + zr[i, 1]
            cp_z(2, q_out, i, z3_b).start()
            cp_z(2, q_out, i, z3_a).start()

    def step_z3(i):
        @pl.when(gets_3)
        def _():
            got_z(2, i).wait_recv()
        hand_over(zr, i, 2)

    def local(h):
        load(2, h, 0).wait()

        @pl.when(h == 0)
        def _():
            lam_copy.wait()
        queries = [qv[h, p * TILE:(p + 1) * TILE, :] for p in range(4)]
        scores = [nt(kv[h, p * TILE:(p + 1) * TILE, :], queries[p]) for p in range(4)]
        blocks = {p: nt(lst[h, n], queries[p]) for n, p in enumerate((1, 3))}
        halves = {p: nt(lst[h, 2], queries[p]) for p in (2, 3)}
        for p in range(4):
            at = p * TILE
            score = scores[p]
            rows = [lamv[l, pl.ds(h, 1), at:at + TILE] for l in range(LOCAL_BITS + 1)]
            mix_a = diagonal_mixing([row[:, :128] for row in rows[:8]])
            mix_b = diagonal_mixing([row[:, 128:] for row in rows[:8]])
            top = jnp.concatenate(
                [score[:128, :128] * mix_a, score[:128, 128:] * rows[8][:, 128:]], axis=1).astype(BF16)
            low_part = jnp.concatenate(
                [jnp.zeros((128, 128), BF16), (score[128:, 128:] * mix_b).astype(BF16)], axis=1)
            weighted = jnp.concatenate([top, low_part], axis=0)
            total = nn(vt[h, :, at:at + TILE], weighted)
            if p in blocks:
                total = total + rows[9] * blocks[p]
            if p in halves:
                total = total + rows[10] * halves[p]
            acc[h, :, :, at:at + TILE] = total.reshape(PARTS, ROWS, TILE)

    def distant(states_there, h, first, totals):
        rows = totals[0].shape[0]
        products = [nt(states_there, qv[h, p * TILE:(p + 1) * TILE, :]) for p in range(4)]
        for p in range(4):
            total = totals[p]
            for n in range(states_there.shape[0] // rows):
                row = lamv[LOCAL_BITS + 1 + first + n, pl.ds(h, 1), p * TILE:(p + 1) * TILE]
                total = total + products[p][n * rows:(n + 1) * rows] * row
            yield p, total

    def near_buckets(h):
        held = [acc[h, :, :, p * TILE:(p + 1) * TILE].reshape(HEAD, TILE) for p in range(4)]
        for p, total in distant(bk[h, 0:5].reshape(5 * HEAD, HEAD), h, 0, held):
            acc[h, :, :, p * TILE:(p + 1) * TILE] = total.reshape(PARTS, ROWS, TILE)

    def far_buckets(i):
        part = i % PARTS
        for n in range(2):
            h = 2 * (i // PARTS) + n
            held = [acc[h, part, :, p * TILE:(p + 1) * TILE] for p in range(4)]
            for p, total in distant(bk[h, 5:8, part].reshape(3 * ROWS, HEAD), h, 5, held):
                out[h, part, :, p * TILE:(p + 1) * TILE] = total.astype(BF16)

    def when_in(t, at, count):
        return jnp.logical_and(t >= at, t < at + count)

    def step(t, carry):
        def stage(at, run, count=ITEMS):
            @pl.when(when_in(t, at, count))
            def _():
                run(t - at)

        def spread(at, run):
            @pl.when(jnp.logical_and(when_in(t, at, HEADS * STRIDE), (t - at) % STRIDE == 0))
            def _():
                run((t - at) // STRIDE)

        def f1(i):
            take_over(i, 0)
            take_over(i, 1)

        def f2(i):
            take_over(i, 2)
            far_buckets(i)

        stage(AT_X, step_x)
        stage(AT_Z3, step_z3)
        stage(AT_Z2, step_z2)
        stage(AT_Y, step_y)
        stage(AT_Z1, step_z1)
        stage(AT_C, step_c)

        @pl.when(jnp.logical_and(t % PARTS == 0, t < ITEMS))
        def _():
            for n in range(2):
                g = 2 * (t // PARTS) + n
                states(g)
                cp_core(g).start()

        stage(AT_F1, f1)
        stage(AT_F2, f2)
        early = jnp.logical_and(jnp.logical_and(t >= AT_L, t < AT_L + 6), (t - AT_L) % 2 == 0)
        late = when_in(t, AT_L + 5, HEADS - 3)

        @pl.when(jnp.logical_or(early, late))
        def _():
            local(jnp.where(early, (t - AT_L) // 2, t - AT_L - 2))
        spread(AT_R, near_buckets)
        return carry

    states(0)
    states(1)
    pl.semaphore_wait(barrier, len(peers))
    cp_core(0).start()
    cp_core(1).start()
    lax.fori_loop(1, STEPS, step, 0)

    remote(st, st, core_s.at[0], core_r.at[0], mate).wait_send()
    remote(xb.at[:, pl.ds(0, 3)], xb.at[:, pl.ds(0, 3)], x_s.at[0], x_r.at[0], at_x(1)).wait_send()
    remote(yb.at[:, pl.ds(0, 3)], yb.at[:, pl.ds(0, 3)], y_s.at[0], y_r.at[0], at_y(1)).wait_send()

    @pl.when(sends_1)
    def _():
        sent_z(0, zo).wait_send()

    @pl.when(sends_2)
    def _():
        sent_z(1, sx).wait_send()

    @pl.when(sends_2b)
    def _():
        sent_z(1, zo).wait_send()

    @pl.when(sends_3)
    def _():
        sent_z(2, sx).wait_send()
    remote(fwd, fwd, f_s.at[0], f_r.at[0, 0], mate).wait_send()


def layer(queries, keys, values, level_weights, out_weight):
    item = (ROWS, HEAD)
    dma = pltpu.SemaphoreType.DMA
    scratch = [
        pltpu.VMEM((HEADS, TOK, HEAD), BF16),
        pltpu.VMEM((HEADS, TOK, HEAD), BF16),
        pltpu.VMEM((HEADS, TOK, HEAD), BF16),
        pltpu.VMEM(level_weights.shape, F32),
        pltpu.VMEM((HEADS, HEAD, TOK), BF16),
        pltpu.VMEM((HEADS, PARTS) + item, F32),
        pltpu.VMEM((HEADS, PARTS) + item, F32),
        pltpu.VMEM((ITEMS, 4) + item, F32),
        pltpu.VMEM((ITEMS, 2) + item, F32),
        pltpu.VMEM((ITEMS, 4) + item, F32),
        pltpu.VMEM((ITEMS, 2) + item, F32),
        pltpu.VMEM((ITEMS,) + item, F32),
        pltpu.VMEM((ITEMS, 3) + item, F32),
        pltpu.VMEM((ITEMS,) + item, F32),
        pltpu.VMEM((ITEMS,) + item, F32),
        pltpu.VMEM((ITEMS, 7) + item, F32),
        pltpu.VMEM((HEADS, 8, PARTS) + item, BF16),
        pltpu.VMEM((HEADS, 3, HEAD, HEAD), BF16),
        pltpu.VMEM((HEADS, PARTS, ROWS, TOK), F32),
        dma((3, HEADS)), dma((1,)),
        dma((1,)), dma((HEADS // 2,)),
        dma((1,)), dma((ITEMS,)),
        dma((1,)), dma((ITEMS,)),
        dma((3,)), dma((ITEMS, 3)),
        dma((1,)), dma((ITEMS, 3)),
    ]
    attended = pl.pallas_call(
        kernel,
        out_shape=pltpu.VMEM((HEADS, PARTS, ROWS, TOK), BF16),
        in_specs=[pl.BlockSpec(memory_space=pl.ANY)] * 4,
        out_specs=pl.BlockSpec(memory_space=pltpu.VMEM),
        scratch_shapes=scratch,
        compiler_params=pltpu.CompilerParams(
            collective_id=0, has_side_effects=True, vmem_limit_bytes=VMEM_MIB << 20),
    )(*[pltpu.with_memory_space_constraint(a, pltpu.HBM) for a in (queries, keys, values, level_weights)])
    return lax.dot_general(
        attended.reshape(HEADS * HEAD, TOK), out_weight, (((0,), (0,)), ((), ())), preferred_element_type=F32).astype(BF16)


def solution(mesh):
    rows = P(("outer", "inner"), None)
    in_specs = (rows, rows, rows, P(None, None, ("outer", "inner")), P())
    return jax.shard_map(layer, mesh=mesh, in_specs=in_specs, out_specs=rows, check_vma=False)
```

```python
import jax
import jax.numpy as jnp
from jax import lax
from jax.experimental import pallas as pl
from jax.experimental.pallas import tpu as pltpu
from jax.sharding import PartitionSpec as P

HEADS = 8
HEAD = 128
LOCAL_BITS = 10
TOK = 1024
TILE = 256
VMEM_MIB = 50
PARTS = 2
ITEMS = 4 * PARTS
ROWS = HEAD // PARTS
STRIDE = PARTS // 2
MESH = pl.DeviceIdType.MESH
F32 = jnp.float32
BF16 = jnp.bfloat16

AT_C = 1
AT_X = 4
AT_Y = 7
AT_F1 = 9
AT_Z1 = 9
AT_Z2 = 12
AT_Z3 = 15
AT_F2 = 16
AT_L = 3
AT_R = 12
STEPS = ITEMS + AT_F2


def nt(a, b):
    return lax.dot_general(a, b, (((1,), (1,)), ((), ())), preferred_element_type=F32)


def nn(a, b):
    return jnp.dot(a, b, preferred_element_type=F32)


def bit_length(values, bits):
    count = jnp.zeros(values.shape, jnp.int32)
    for shift in range(bits):
        count = count + (jnp.right_shift(values, shift) > 0).astype(jnp.int32)
    return count


def diagonal_mixing(lam):
    group = lax.broadcasted_iota(jnp.int32, (16, 128), 0)
    token16 = lax.broadcasted_iota(jnp.int32, (16, 128), 1)
    far = bit_length(jnp.bitwise_xor(group, jnp.right_shift(token16, 3)), 4)
    coarse = jnp.where(far == 1, lam[4], jnp.where(far == 2, lam[5], jnp.where(far == 3, lam[6], lam[7])))
    coarse = jnp.where(group < jnp.right_shift(token16, 3), coarse, 0.0)
    row = lax.broadcasted_iota(jnp.int32, (8, 128), 0)
    token8 = jnp.bitwise_and(lax.broadcasted_iota(jnp.int32, (8, 128), 1), 7)
    near = bit_length(jnp.bitwise_xor(row, token8), 3)
    fine = jnp.where(near == 0, lam[0], jnp.where(near == 1, lam[1], jnp.where(near == 2, lam[2], lam[3])))
    fine = jnp.where(row <= token8, fine, 0.0)
    major = lax.broadcasted_iota(jnp.int32, (16, 8, 128), 0)
    token = lax.broadcasted_iota(jnp.int32, (16, 8, 128), 2)
    spread = jnp.broadcast_to(coarse[:, None, :], (16, 8, 128))
    return jnp.where(jnp.right_shift(token, 3) == major, fine[None], spread).reshape(128, 128)


def kernel(
    q_hbm, k_hbm, v_hbm, lam_hbm, out,
    qv, kv, vv, lamv, vt, st, ps, xb, sx, yb, sy, zo, zr, p_out, q_out, fwd, bk, lst, acc,
    load_sem, whole_sem, core_s, core_r, x_s, x_r, y_s, y_r, z_s, z_r, f_s, f_r,
):
    z = lax.axis_index("outer")
    inner = lax.axis_index("inner")
    c = inner % 2
    x = (inner // 2) % 4
    y = inner // 8

    def device(z_to, y_to, x_to, c_to):
        return (z_to, (y_to * 4 + x_to) * 2 + c_to)

    mate = device(z, y, x, 1 - c)

    def load(kind, h, source_h):
        source, target = ((k_hbm, kv), (v_hbm, vv), (q_hbm, qv))[kind]
        return pltpu.make_async_copy(
            source.at[:, pl.ds(source_h * HEAD, HEAD)], target.at[h], load_sem.at[kind, h])

    lam_copy = pltpu.make_async_copy(lam_hbm, lamv, whole_sem.at[0])

    for h in range(HEADS):
        load(0, h, h).start()
        load(1, h, h).start()
    lam_copy.start()
    for h in range(HEADS):
        load(2, h, h).start()

    barrier = pltpu.get_barrier_semaphore()
    peers = [mate]
    peers += [device(z, y, (x + d) % 4, c) for d in (1, 2, 3)]
    peers += [device(z, (y + d) % 4, x, c) for d in (1, 2, 3)]
    peers += [device((z + d) % 8, y, x, c) for d in (1, 7, 2, 6)]
    for peer in peers:
        pl.semaphore_signal(barrier, inc=1, device_id=peer, device_id_type=MESH)

    def remote(src, dst, send, recv, to):
        return pltpu.make_async_remote_copy(
            src_ref=src, dst_ref=dst, send_sem=send, recv_sem=recv, device_id=to, device_id_type=MESH)

    def at_x(d):
        return device(z, y, (x + d) % 4, c)

    def at_y(d):
        return device(z, (y + d) % 4, x, c)

    def at_z(to):
        return device(to, y, x, c)

    def cp_core(h):
        return remote(st.at[h], ps.at[h], core_s.at[0], core_r.at[h], mate)

    def take_core(g):
        cp_core(g).wait_recv()
        bk[g, 0] = jnp.where(c == 1, ps[g], 0.0).astype(BF16)

    def cp_x(i, d):
        return remote(xb.at[i, x], xb.at[i, x], x_s.at[0], x_r.at[i], at_x(d))

    def got_x(i):
        return remote(xb.at[i, pl.ds(0, 3)], xb.at[i, pl.ds(0, 3)], x_s.at[0], x_r.at[i], at_x(1))

    def cp_y(i, d):
        return remote(yb.at[i, y], yb.at[i, y], y_s.at[0], y_r.at[i], at_y(d))

    def got_y(i):
        return remote(yb.at[i, pl.ds(0, 3)], yb.at[i, pl.ds(0, 3)], y_s.at[0], y_r.at[i], at_y(1))

    x_pair = x + 1 - 2 * (x % 2)
    y_pair = y + 1 - 2 * (y % 2)
    z_pair = z + 1 - 2 * (z % 2)
    low = z % 4
    sends_1 = jnp.logical_or(z < 4, z % 2 == 0)
    gets_1 = jnp.logical_or(z < 4, z % 2 == 1)
    sends_2 = low == 1
    sends_2b = z == 2
    gets_2 = jnp.logical_or(low >= 2, z == 0)
    sends_3 = jnp.logical_or(z == 0, z == 3)
    gets_3 = z >= 4
    z3_a = jnp.where(z == 0, 7, 4)
    z3_b = jnp.where(z == 0, 6, 5)

    def cp_z(n, source, i, to):
        return remote(source.at[i], zr.at[i, n], z_s.at[n], z_r.at[i, n], at_z(to))

    def got_z(n, i):
        return remote(zr.at[i, n], zr.at[i, n], z_s.at[n], z_r.at[i, n], at_z(z_pair))

    def sent_z(n, source):
        return remote(source, source, z_s.at[n], z_r.at[0, n], at_z(z_pair))

    has = (x % 2 == 1, x >= 2, y % 2 == 1, y >= 2, z % 2 == 1, low >= 2, z >= 4)
    places = ((0, 2), (2, 2), (4, 3))

    def cp_f(source, i, kind):
        first, count = places[kind]
        return remote(source.at[i], fwd.at[i, pl.ds(first, count)], f_s.at[0], f_r.at[i, kind], mate)

    def keep(h, i, n, value):
        bk[h, 1 + n, i % PARTS] = jnp.where(has[n], value, 0.0).astype(BF16)

    def hand_over(source, i, kind):
        cp_f(source, i, kind).start()
        first, count = places[kind]
        for n in range(count):
            keep(2 * (i // PARTS) + c, i, first + n, source[i, n])

    def take_over(i, kind):
        first, count = places[kind]
        there = fwd.at[i, pl.ds(first, count)]
        remote(there, there, f_s.at[0], f_r.at[i, kind], mate).wait_recv()
        for n in range(count):
            keep(2 * (i // PARTS) + 1 - c, i, first + n, fwd[i, first + n])

    def states(h):
        load(0, h, 0).wait()
        load(1, h, 0).wait()
        vt[h] = jnp.transpose(vv[h])
        part = []
        for p in range(4):
            part.append(nn(vt[h, :, p * TILE:(p + 1) * TILE], kv[h, p * TILE:(p + 1) * TILE, :]))
        first = part[0] + part[1]
        lst[h, 0] = part[0].astype(BF16)
        lst[h, 1] = part[2].astype(BF16)
        lst[h, 2] = first.astype(BF16)
        st[h] = (first + (part[2] + part[3])).reshape(PARTS, ROWS, HEAD)

    def step_c(i):
        h = 2 * (i // PARTS) + c

        @pl.when(i % PARTS == 0)
        def _():
            take_core(h)

        @pl.when(i % PARTS == PARTS - 1)
        def _():
            take_core(2 * (i // PARTS) + 1 - c)

        xb[i, x] = st[h, i % PARTS] + ps[h, i % PARTS]
        for d in (2, 1, 3):
            cp_x(i, d).start()

    def step_x(i):
        got_x(i).wait_recv()
        front = xb[i, 0] + xb[i, 1]
        yb[i, y] = front + (xb[i, 2] + xb[i, 3])
        for d in (2, 1, 3):
            cp_y(i, d).start()
        sx[i, 0] = xb[i, x_pair]
        sx[i, 1] = front
        hand_over(sx, i, 0)

    def step_y(i):
        got_y(i).wait_recv()
        front = yb[i, 0] + yb[i, 1]
        zo[i] = front + (yb[i, 2] + yb[i, 3])

        @pl.when(sends_1)
        def _():
            cp_z(0, zo, i, z_pair).start()
        sy[i, 0] = yb[i, y_pair]
        sy[i, 1] = front
        hand_over(sy, i, 1)

    def step_z1(i):
        @pl.when(gets_1)
        def _():
            got_z(0, i).wait_recv()
            p_out[i] = zo[i] + zr[i, 0]

        @pl.when(sends_2)
        def _():
            cp_z(1, p_out, i, z + 2).start()
            cp_z(1, p_out, i, z + 1).start()

        @pl.when(sends_2b)
        def _():
            cp_z(1, p_out, i, 0).start()

    def step_z2(i):
        @pl.when(gets_2)
        def _():
            got_z(1, i).wait_recv()

        @pl.when(sends_3)
        def _():
            q_out[i] = p_out[i] + zr[i, 1]
            cp_z(2, q_out, i, z3_b).start()
            cp_z(2, q_out, i, z3_a).start()

    def step_z3(i):
        @pl.when(gets_3)
        def _():
            got_z(2, i).wait_recv()
        hand_over(zr, i, 2)

    def local(h):
        load(2, h, 0).wait()

        @pl.when(h == 0)
        def _():
            lam_copy.wait()
        queries = [qv[h, p * TILE:(p + 1) * TILE, :] for p in range(4)]
        scores = [nt(kv[h, p * TILE:(p + 1) * TILE, :], queries[p]) for p in range(4)]
        blocks = {p: nt(lst[h, n], queries[p]) for n, p in enumerate((1, 3))}
        halves = {p: nt(lst[h, 2], queries[p]) for p in (2, 3)}
        for p in range(4):
            at = p * TILE
            score = scores[p]
            rows = [lamv[l, pl.ds(h, 1), at:at + TILE] for l in range(LOCAL_BITS + 1)]
            mix_a = diagonal_mixing([row[:, :128] for row in rows[:8]])
            mix_b = diagonal_mixing([row[:, 128:] for row in rows[:8]])
            top = jnp.concatenate(
                [score[:128, :128] * mix_a, score[:128, 128:] * rows[8][:, 128:]], axis=1).astype(BF16)
            low_part = jnp.concatenate(
                [jnp.zeros((128, 128), BF16), (score[128:, 128:] * mix_b).astype(BF16)], axis=1)
            weighted = jnp.concatenate([top, low_part], axis=0)
            total = nn(vt[h, :, at:at + TILE], weighted)
            if p in blocks:
                total = total + rows[9] * blocks[p]
            if p in halves:
                total = total + rows[10] * halves[p]
            acc[h, :, :, at:at + TILE] = total.reshape(PARTS, ROWS, TILE)

    def distant(states_there, h, first, totals):
        rows = totals[0].shape[0]
        products = [nt(states_there, qv[h, p * TILE:(p + 1) * TILE, :]) for p in range(4)]
        for p in range(4):
            total = totals[p]
            for n in range(states_there.shape[0] // rows):
                row = lamv[LOCAL_BITS + 1 + first + n, pl.ds(h, 1), p * TILE:(p + 1) * TILE]
                total = total + products[p][n * rows:(n + 1) * rows] * row
            yield p, total

    def near_buckets(h):
        held = [acc[h, :, :, p * TILE:(p + 1) * TILE].reshape(HEAD, TILE) for p in range(4)]
        for p, total in distant(bk[h, 0:5].reshape(5 * HEAD, HEAD), h, 0, held):
            acc[h, :, :, p * TILE:(p + 1) * TILE] = total.reshape(PARTS, ROWS, TILE)

    def far_buckets(i):
        part = i % PARTS
        for n in range(2):
            h = 2 * (i // PARTS) + n
            held = [acc[h, part, :, p * TILE:(p + 1) * TILE] for p in range(4)]
            for p, total in distant(bk[h, 5:8, part].reshape(3 * ROWS, HEAD), h, 5, held):
                out[h, part, :, p * TILE:(p + 1) * TILE] = total.astype(BF16)

    def when_in(t, at, count):
        return jnp.logical_and(t >= at, t < at + count)

    def step(t, carry):
        def stage(at, run, count=ITEMS):
            @pl.when(when_in(t, at, count))
            def _():
                run(t - at)

        def spread(at, run):
            @pl.when(jnp.logical_and(when_in(t, at, HEADS * STRIDE), (t - at) % STRIDE == 0))
            def _():
                run((t - at) // STRIDE)

        def f1(i):
            take_over(i, 0)
            take_over(i, 1)

        def f2(i):
            take_over(i, 2)
            far_buckets(i)

        stage(AT_X, step_x)
        stage(AT_Z3, step_z3)
        stage(AT_Z2, step_z2)
        stage(AT_Y, step_y)
        stage(AT_Z1, step_z1)
        stage(AT_C, step_c)

        @pl.when(jnp.logical_and(t % PARTS == 0, t < ITEMS))
        def _():
            for n in range(2):
                g = 2 * (t // PARTS) + (1 - c if n == 0 else c)
                states(g)
                cp_core(g).start()

        stage(AT_F1, f1)
        stage(AT_F2, f2)
        early = jnp.logical_and(jnp.logical_and(t >= AT_L, t < AT_L + 6), (t - AT_L) % 2 == 0)
        late = when_in(t, AT_L + 5, HEADS - 3)

        @pl.when(jnp.logical_or(early, late))
        def _():
            local(jnp.where(early, (t - AT_L) // 2, t - AT_L - 2))
        spread(AT_R, near_buckets)
        return carry

    states(1 - c)
    pl.semaphore_wait(barrier, len(peers))
    cp_core(1 - c).start()
    states(c)
    cp_core(c).start()
    lax.fori_loop(1, STEPS, step, 0)

    remote(st, st, core_s.at[0], core_r.at[0], mate).wait_send()
    remote(xb.at[:, pl.ds(0, 3)], xb.at[:, pl.ds(0, 3)], x_s.at[0], x_r.at[0], at_x(1)).wait_send()
    remote(yb.at[:, pl.ds(0, 3)], yb.at[:, pl.ds(0, 3)], y_s.at[0], y_r.at[0], at_y(1)).wait_send()

    @pl.when(sends_1)
    def _():
        sent_z(0, zo).wait_send()

    @pl.when(sends_2)
    def _():
        sent_z(1, sx).wait_send()

    @pl.when(sends_2b)
    def _():
        sent_z(1, zo).wait_send()

    @pl.when(sends_3)
    def _():
        sent_z(2, sx).wait_send()
    remote(fwd, fwd, f_s.at[0], f_r.at[0, 0], mate).wait_send()


def layer(queries, keys, values, level_weights, out_weight):
    item = (ROWS, HEAD)
    dma = pltpu.SemaphoreType.DMA
    scratch = [
        pltpu.VMEM((HEADS, TOK, HEAD), BF16),
        pltpu.VMEM((HEADS, TOK, HEAD), BF16),
        pltpu.VMEM((HEADS, TOK, HEAD), BF16),
        pltpu.VMEM(level_weights.shape, F32),
        pltpu.VMEM((HEADS, HEAD, TOK), BF16),
        pltpu.VMEM((HEADS, PARTS) + item, F32),
        pltpu.VMEM((HEADS, PARTS) + item, F32),
        pltpu.VMEM((ITEMS, 4) + item, F32),
        pltpu.VMEM((ITEMS, 2) + item, F32),
        pltpu.VMEM((ITEMS, 4) + item, F32),
        pltpu.VMEM((ITEMS, 2) + item, F32),
        pltpu.VMEM((ITEMS,) + item, F32),
        pltpu.VMEM((ITEMS, 3) + item, F32),
        pltpu.VMEM((ITEMS,) + item, F32),
        pltpu.VMEM((ITEMS,) + item, F32),
        pltpu.VMEM((ITEMS, 7) + item, F32),
        pltpu.VMEM((HEADS, 8, PARTS) + item, BF16),
        pltpu.VMEM((HEADS, 3, HEAD, HEAD), BF16),
        pltpu.VMEM((HEADS, PARTS, ROWS, TOK), F32),
        dma((3, HEADS)), dma((1,)),
        dma((1,)), dma((HEADS,)),
        dma((1,)), dma((ITEMS,)),
        dma((1,)), dma((ITEMS,)),
        dma((3,)), dma((ITEMS, 3)),
        dma((1,)), dma((ITEMS, 3)),
    ]
    attended = pl.pallas_call(
        kernel,
        out_shape=pltpu.VMEM((HEADS, PARTS, ROWS, TOK), BF16),
        in_specs=[pl.BlockSpec(memory_space=pl.ANY)] * 4,
        out_specs=pl.BlockSpec(memory_space=pltpu.VMEM),
        scratch_shapes=scratch,
        compiler_params=pltpu.CompilerParams(
            collective_id=0, has_side_effects=True, vmem_limit_bytes=VMEM_MIB << 20),
    )(*[pltpu.with_memory_space_constraint(a, pltpu.HBM) for a in (queries, keys, values, level_weights)])
    return lax.dot_general(
        attended.reshape(HEADS * HEAD, TOK), out_weight, (((0,), (0,)), ((), ())), preferred_element_type=F32).astype(BF16)


def solution(mesh):
    rows = P(("outer", "inner"), None)
    in_specs = (rows, rows, rows, P(None, None, ("outer", "inner")), P())
    return jax.shard_map(layer, mesh=mesh, in_specs=in_specs, out_specs=rows, check_vma=False)
```
